32 devices in a mesh: dp: 8 (over z, x), mp: 4 (over y, core).
Axes of the slice: x: 2, y: 2, z: 4, core: 2. Of those that a mesh axis runs over, the one named last changes fastest.
Arguments:
- hidden_in: float32 [8192, 1024], P(('dp', 'mp'))
- cotangent: float32 [8192, 1024], P(('dp', 'mp')), may hold values from -6 to 6
- lengths: int32 [8, 3], P('dp'), may hold values from 1 to 512, 1024 in all within a row
- ln_gain: bfloat16 [2, 1024], replicated, may hold values from 0.5 to 1.5
- ln_bias: bfloat16 [2, 1024], replicated, may hold values from -1.5 to 1.5
- qkv_weight: bfloat16 [2, 1024, 3072], replicated, may hold values from -0.1875 to 0.1875
- qkv_bias: bfloat16 [2, 3072], replicated, may hold values from -1.5 to 1.5
- out_weight: bfloat16 [2, 1024, 1024], replicated, may hold values from -0.75 to 0.75
- out_bias: bfloat16 [2, 1024], replicated, may hold values from -1.5 to 1.5
- fc_weight: bfloat16 [2, 1024, 4096], P(None, None, 'mp'), may hold values from -0.1875 to 0.1875
- fc_bias: bfloat16 [2, 4096], P(None, 'mp'), may hold values from -1.5 to 1.5
- proj_weight: bfloat16 [2, 1024, 4096], P(None, None, 'mp'), may hold values from -0.09375 to 0.09375
- proj_bias: bfloat16 [2, 1024], replicated, may hold values from -1.5 to 1.5
Outputs:
- hidden_out: float32 [8192, 1024], P(('dp', 'mp'))
- grad_in: float32 [8192, 1024], P(('dp', 'mp'))
- stats: float32 [2, 3], replicated
- grad_ln_gain: float32 [2, 1024], replicated
- grad_ln_bias: float32 [2, 1024], replicated
- grad_qkv_weight: float32 [2, 1024, 3072], P(None, 'dp')
- grad_qkv_bias: float32 [2, 3072], replicated
- grad_out_weight: float32 [2, 1024, 1024], P(None, 'dp')
- grad_out_bias: float32 [2, 1024], replicated
- grad_fc_weight: float32 [2, 1024, 4096], P(None, 'dp', 'mp')
- grad_fc_bias: float32 [2, 4096], P(None, 'mp')
- grad_proj_weight: float32 [2, 1024, 4096], P(None, 'dp', 'mp')
- grad_proj_bias: float32 [2, 1024], replicated
The draws below stay inside these ranges and needn't reach their ends.
Inputs may be any that keep to these rules, and one draw needn't show every extreme that they name: Row g lists, in order, the lengths of the sequences of token group g; each row sums to 1024 and its largest entry is 512.
All inputs are finite; a program needn't handle non-finite values.
Results may differ from the reference program's by a relative error of at most 0.019.
Values may be sent and summed in bfloat16 or wider, within the bound.
No kernel may reach another device: no remote copies, remote signals or barrier semaphores. Data moves between devices by JAX's collectives and lax.ppermute only.
A program may use at most 256 MiB of HBM per device.

```python
import math
import jax
import jax.numpy as jnp
import numpy as np
from jax import lax

D = 1024
HEADS = 16
HEAD_DIM = 64
ROT_DIM = 16
FF = 4096
LAYERS = 2
TOK_DEV = 256
GROUP_TOK = 1024
SEQS = 3
MAXLEN = 512
TOKENS = 8192
N_DP = 8
N_MP = 4


def draw_hidden_in(key, part):
    key_one = jax.random.fold_in(key, 0)
    normal_draw = jax.random.normal(key_one, (TOKENS, D), jnp.float32)
    row_ramp = jnp.exp(jnp.arange(TOKENS, dtype=jnp.float32) * (math.log(3.0) / TOKENS))
    return normal_draw * row_ramp[:, None]


def shard_levels(rng, shape, cuts, smallest, largest):
    factor_of, own = 1.0, jax.random.fold_in(rng, 6)
    for dim, shards_of in cuts:
        heights = jnp.exp(jax.random.uniform(jax.random.fold_in(own, dim), (shards_of,), jnp.float32, smallest / len(cuts), largest / len(cuts)))
        factor_of = factor_of * jnp.repeat(heights, shape[dim] // shards_of).reshape([-1 if axis == dim else 1 for axis in range(len(shape))])
    return factor_of


def profile(count, total, most, skew):
    portions = [(1 << 20) // math.isqrt(grade ** skew) + 1 for grade in range(2, count + 1)]
    spare, holding = total - most - (count - 1), [1] * (count - 1)
    while spare > 0:
        free = [i for i in range(count - 1) if holding[i] < most]
        mass, remaining = sum([portions[i] for i in free]), spare
        for i in free:
            extra = min(most - holding[i], max(1, remaining * portions[i] // mass), spare)
            holding[i] = holding[i] + extra
            spare = spare - extra
    return np.array([most] + holding)


def uneven(rng, number_of, total, limit, skew):
    if number_of == 2:
        one = jax.random.randint(rng, (), max(1, total - limit), min(limit, total - 1) + 1)
        return jnp.stack([one, total - one])
    sizes = jnp.asarray(profile(number_of, total, limit, skew), jnp.int32)
    twos = (number_of - 1) // 2
    giver, receiver = sizes[1:1 + 2 * twos:2], sizes[2:2 + 2 * twos:2]
    room = jnp.minimum(giver - 1, limit - receiver)
    moved = jax.random.randint(jax.random.fold_in(rng, 1), (twos,), 0, 1 << 20) % (room + 1)
    sizes = sizes.at[1:1 + 2 * twos:2].set(giver - moved).at[2:2 + 2 * twos:2].set(receiver + moved)
    return sizes[jax.random.permutation(jax.random.fold_in(rng, 2), number_of)]


def centred(stream_key, extent, width, reach, shards=(), kind=jnp.bfloat16):
    array = width * jax.random.normal(stream_key, extent, jnp.float32)
    if shards:
        array = array * shard_levels(stream_key, extent, shards, -0.22, 0.18)
    return jnp.clip(array, -reach, reach).astype(kind)


def setup_inputs(seed: int = 0) -> dict:
    key_of = jax.random.split(jax.random.key(seed), 14)
    hidden_in = draw_hidden_in(jax.random.fold_in(key_of[13], 71), 0)
    cotangent = centred(key_of[1], (TOKENS, D), 1.0, 6.0, ((0, 32),), jnp.float32)
    lengths = jax.vmap(lambda own: uneven(own, SEQS, GROUP_TOK, MAXLEN, 2))(jax.random.split(key_of[2], N_DP)).reshape((N_DP, SEQS)).astype(jnp.int32)
    ln_gain = jnp.clip(1.0 + 0.1 * jax.random.normal(key_of[3], (LAYERS, D), jnp.float32), 0.5, 1.5).astype(jnp.bfloat16)
    ln_bias = centred(key_of[4], (LAYERS, D), 0.3, 1.5)
    qkv_weight = centred(key_of[5], (LAYERS, D, 3 * D), D ** -0.5, 0.1875)
    qkv_bias = centred(key_of[6], (LAYERS, 3 * D), 0.3, 1.5)
    out_weight = centred(key_of[7], (LAYERS, D, D), (D // 16) ** -0.5, 0.75)
    out_bias = centred(key_of[8], (LAYERS, D), 0.3, 1.5)
    fc_weight = centred(key_of[9], (LAYERS, D, FF), D ** -0.5, 0.1875, ((2, 4),))
    fc_bias = centred(key_of[10], (LAYERS, FF), 0.3, 1.5, ((1, 4),))
    proj_weight = centred(key_of[11], (LAYERS, D, FF), FF ** -0.5, 0.09375, ((2, 4),))
    proj_bias = centred(key_of[12], (LAYERS, D), 0.3, 1.5)
    return dict(hidden_in=hidden_in, cotangent=cotangent, lengths=lengths, ln_gain=ln_gain, ln_bias=ln_bias, qkv_weight=qkv_weight, qkv_bias=qkv_bias, out_weight=out_weight, out_bias=out_bias, fc_weight=fc_weight, fc_bias=fc_bias, proj_weight=proj_weight, proj_bias=proj_bias)


EPS = 1e-05
NEG = -1e+30
HIGH = lax.Precision.HIGHEST

@jax.custom_vjp
def low(v):
    return lax.optimization_barrier(v.astype(jnp.bfloat16)).astype(jnp.float32)

@jax.custom_vjp
def low_back(v):
    return v

def low_keep(v):
    return (low(v), None)

def low_pass(kept, grad):
    return (grad,)

def back_keep(v):
    return (v, None)

def back_low(kept, grad):
    return (low(grad),)
low.defvjp(low_keep, low_pass)
low_back.defvjp(back_keep, back_low)

def norm_rows(hidden, gain, shift):
    center = hidden - lax.optimization_barrier(jnp.mean(hidden, axis=-1, keepdims=True))
    spread = lax.optimization_barrier(jnp.mean(center * center, axis=-1, keepdims=True))
    return center * lax.rsqrt(spread + EPS) * gain + shift

def seq_layout(seq_lengths, row_ids):
    ends = jnp.cumsum(seq_lengths).astype(jnp.int32)
    starts = (ends - seq_lengths).astype(jnp.int32)
    segment = lax.optimization_barrier(jnp.sum((row_ids[:, None] >= ends[None, :]).astype(jnp.int32), axis=1)).astype(jnp.int32)
    begins = lax.optimization_barrier(jnp.max(jnp.where(starts[None, :] <= row_ids[:, None], starts[None, :], 0), axis=1)).astype(jnp.int32)
    return (segment, (row_ids - begins).astype(jnp.int32))

def angles(positions):
    half_rot = ROT_DIM // 2
    frequency = jnp.exp(jnp.arange(half_rot, dtype=jnp.float32) * (-2.0 * math.log(10000.0) / ROT_DIM))
    angle_grid = positions.astype(jnp.float32)[:, None] * frequency[None, :]
    return (jnp.cos(angle_grid)[:, None, :], jnp.sin(angle_grid)[:, None, :])

def rotate(vectors, cosine_table, sine_table):
    half_rot = ROT_DIM // 2
    first_half = vectors[..., :half_rot]
    second = vectors[..., half_rot:ROT_DIM]
    return jnp.concatenate([first_half * cosine_table - second * sine_table, second * cosine_table + first_half * sine_table, vectors[..., ROT_DIM:]], axis=-1)

def matmul(left, right):
    return jnp.dot(left, right, precision=HIGH)

def attend(query_all, key_all, value_all, segment):
    total_rows = query_all.shape[0]
    query_block = min(512, total_rows)
    score_scale = 1.0 / math.sqrt(HEAD_DIM)
    key_rows = jnp.arange(total_rows, dtype=jnp.int32)

    def one_block(blk_idx):
        blk_start = blk_idx * query_block
        query_blk = lax.dynamic_slice_in_dim(query_all, blk_start, query_block, 0)
        query_seg = lax.dynamic_slice_in_dim(segment, blk_start, query_block, 0)
        query_rows = blk_start + jnp.arange(query_block, dtype=jnp.int32)
        scores = low_back(jnp.einsum('qhd,khd->hqk', query_blk, key_all, precision=HIGH) * score_scale)
        allowed = (query_seg[:, None] == segment[None, :]) & (key_rows[None, :] <= query_rows[:, None])
        scores = jnp.where(allowed[None], scores, NEG)
        prob_blk = low(jax.nn.softmax(scores, axis=-1))
        return jnp.einsum('hqk,khd->qhd', prob_blk, value_all, precision=HIGH)
    outputs = lax.map(jax.checkpoint(one_block), jnp.arange(total_rows // query_block, dtype=jnp.int32))
    return outputs.reshape(total_rows, HEADS, HEAD_DIM)

def group_forward(hidden, params, segment, positions):
    gain_all, shift_all, qkv_w, qkv_b, out_w, out_b, fc_w, fc_b, proj_w, proj_b = params
    total_rows = hidden.shape[0]
    cosine_table, sine_table = angles(positions)
    layer_terms = []
    for layer_idx in range(LAYERS):
        normed = low(norm_rows(hidden, gain_all[layer_idx], shift_all[layer_idx]))
        qkv_lin = low_back(matmul(normed, qkv_w[layer_idx]) + qkv_b[layer_idx]).reshape(total_rows, 3, HEADS, HEAD_DIM)
        query_r = low(rotate(qkv_lin[:, 0], cosine_table, sine_table))
        key_r = low(rotate(qkv_lin[:, 1], cosine_table, sine_table))
        value_r = low(qkv_lin[:, 2])
        mixed = low_back(low(attend(query_r, key_r, value_r, segment))).reshape(total_rows, D)
        attn_out = low_back(matmul(mixed, out_w[layer_idx]) + out_b[layer_idx])
        pre_act = low_back(matmul(normed, fc_w[layer_idx]) + fc_b[layer_idx])
        gelu_out = low(jax.nn.gelu(pre_act, approximate=False))
        ffn_out = low_back(lax.dot_general(gelu_out, proj_w[layer_idx], (((1,), (1,)), ((), ())), precision=HIGH) + proj_b[layer_idx])
        layer_terms.append(jnp.stack([jnp.sum(hidden * hidden), jnp.sum(attn_out * attn_out), jnp.sum(ffn_out * ffn_out)]))
        hidden = hidden + attn_out + ffn_out
    return (hidden, jnp.stack(layer_terms))

def reference(hidden_in, cotangent, lengths, ln_gain, ln_bias, qkv_weight, qkv_bias, out_weight, out_bias, fc_weight, fc_bias, proj_weight, proj_bias):
    params = tuple((item.astype(jnp.float32) for item in (ln_gain, ln_bias, qkv_weight, qkv_bias, out_weight, out_bias, fc_weight, fc_bias, proj_weight, proj_bias)))
    group_size = TOK_DEV * N_MP
    hidden_groups = hidden_in.reshape(N_DP, group_size, D)
    cot_groups = cotangent.reshape(N_DP, group_size, D)
    row_ids = jnp.arange(group_size, dtype=jnp.int32)

    def group_step(totals, inputs):
        hidden_blk, cot_blk, seq_lengths = inputs
        segment, positions = seq_layout(seq_lengths, row_ids)

        def run(hidden_val, param_val):
            return group_forward(hidden_val, param_val, segment, positions)
        out_blk, pull_back, layer_terms = jax.vjp(run, hidden_blk, params, has_aux=True)
        grad_hidden, grad_params = pull_back(cot_blk)
        grad_sum, term_sum = totals
        grad_sum = jax.tree.map(jnp.add, grad_sum, grad_params)
        return ((grad_sum, term_sum + layer_terms), (out_blk, grad_hidden))
    zero_grads = jax.tree.map(jnp.zeros_like, params)
    zero_terms = jnp.zeros((LAYERS, 3), jnp.float32)
    (grad_sum, term_sum), (out_groups, grad_groups) = lax.scan(group_step, (zero_grads, zero_terms), (hidden_groups, cot_groups, lengths))
    stats = jnp.sqrt(term_sum / (TOKENS * D))
    return (out_groups.reshape(TOKENS, D), grad_groups.reshape(TOKENS, D), stats, grad_sum[0], grad_sum[1], grad_sum[2], grad_sum[3], grad_sum[4], grad_sum[5], grad_sum[6], grad_sum[7], grad_sum[8], grad_sum[9])
```

```python
import functools
import math

import jax
import jax.numpy as jnp
from jax import lax
from jax.experimental import pallas as pl
from jax.experimental.pallas import tpu as pltpu
from jax.sharding import PartitionSpec as P

HEADS = 16
HEAD_DIM = 64
ROT_DIM = 16
LAYERS = 2

EPS = 1e-05
NEG = -1e30
LANES = 128
CHUNK = 128


f32 = jnp.float32
bf16 = jnp.bfloat16


def norm_stats(hidden):
    center = hidden - jnp.mean(hidden, axis=-1, keepdims=True)
    spread = jnp.mean(center * center, axis=-1, keepdims=True)
    return center, lax.rsqrt(spread + EPS)


def dot_nn(left, right):
    return lax.dot_general(left, right, (((1,), (0,)), ((), ())), preferred_element_type=f32)


def dot_nt(left, right):
    return lax.dot_general(left, right, (((1,), (1,)), ((), ())), preferred_element_type=f32)


def dot_tn(left, right):
    return lax.dot_general(left, right, (((0,), (0,)), ((), ())), preferred_element_type=f32)


def swap_halves(block):
    lane = lax.broadcasted_iota(jnp.int32, block.shape, 1) % HEAD_DIM
    half = ROT_DIM // 2
    return jnp.where(
        lane < half, pltpu.roll(block, LANES - half, 1), pltpu.roll(block, half, 1)
    )


def head_mask(block, which):
    lane = lax.broadcasted_iota(jnp.int32, block.shape, 1)
    keep = (lane < HEAD_DIM) if which == 0 else (lane >= HEAD_DIM)
    return jnp.where(keep, block, jnp.zeros_like(block))


def fill_bias(bias_ref, begin_ref, blk, low, rows):
    begin = begin_ref[:, blk * rows : (blk + 1) * rows]
    query = blk * rows + lax.broadcasted_iota(jnp.int32, (CHUNK, rows), 1)
    for start in range(low * rows, (blk + 1) * rows, CHUNK):
        key = start + lax.broadcasted_iota(jnp.int32, (CHUNK, rows), 0)
        keep = (key >= begin) & (key <= query)
        bias_ref[start - low * rows : start - low * rows + CHUNK, :] = jnp.where(keep, 0.0, NEG)


def forward_kernel(
    rows, width, window, me_ref, lin_ref, cos_ref, sin_ref, begin_ref,
    out_ref, q_ref, k_ref, v_ref, lse_ref,
    vt_ref, bias_ref, score_ref, prob_ref, ot_ref,
):
    me = me_ref[0]
    group = q_ref.shape[0]
    blocks = group // rows
    reach = window // rows
    pairs = width // LANES
    scale = 1.0 / math.sqrt(HEAD_DIM)
    for blk in range(blocks):
        slot = pl.multiple_of((me ^ blk) * rows, rows)
        here = slice(blk * rows, (blk + 1) * rows)
        cosine, sine = cos_ref[here, :], sin_ref[here, :]
        for part, ref in ((0, q_ref), (1, k_ref)):
            for pair in range(pairs):
                cols = slice(part * width + pair * LANES, part * width + (pair + 1) * LANES)
                block = lin_ref[pl.ds(slot, rows), cols]
                turned = block * cosine + swap_halves(block) * sine
                ref[here, pair * LANES : (pair + 1) * LANES] = turned.astype(bf16)
        value = lin_ref[pl.ds(slot, rows), 2 * width :]
        v_ref[here, :] = value.astype(bf16)
        vt_ref[:, here] = value.T.astype(bf16)
    for blk in range(blocks):
        low = max(0, blk - reach)
        span = (blk + 1 - low) * rows
        slot = pl.multiple_of((me ^ blk) * rows, rows)
        here = slice(blk * rows, (blk + 1) * rows)
        fill_bias(bias_ref, begin_ref, blk, low, rows)
        for head in range(2 * pairs):
            pair = head // 2
            cols = slice(pair * LANES, (pair + 1) * LANES)
            query = head_mask(q_ref[here, cols], head % 2) * jnp.asarray(scale, bf16)
            best = jnp.full((1, rows), NEG, f32)
            for at in range(0, span, CHUNK):
                keys = k_ref[low * rows + at : low * rows + at + CHUNK, cols]
                score = dot_nt(keys, query) + bias_ref[at : at + CHUNK, :]
                score_ref[at : at + CHUNK, :] = score
                best = jnp.maximum(best, jnp.max(score, axis=0, keepdims=True))
            total = jnp.zeros((1, rows), f32)
            for at in range(0, span, CHUNK):
                weight = jnp.exp(score_ref[at : at + CHUNK, :] - best)
                total = total + jnp.sum(weight, axis=0, keepdims=True)
                prob_ref[at : at + CHUNK, :] = weight.astype(bf16)
            mixed = dot_nn(
                vt_ref[head * HEAD_DIM : (head + 1) * HEAD_DIM, low * rows : low * rows + span],
                prob_ref[:span, :],
            )
            ot_ref[head * HEAD_DIM : (head + 1) * HEAD_DIM, :] = mixed * (1.0 / total)
            lse_ref[head : head + 1, here] = best + jnp.log(total)
        out_ref[pl.ds(slot, rows), :] = ot_ref[...].T.astype(bf16)


def backward_kernel(
    rows, width, window, me_ref, do_ref, o_ref, q_ref, k_ref, v_ref, lse_ref,
    cos_ref, sin_ref, begin_ref, dlin_ref,
    kt_ref, bias_ref, prob_ref, ds_ref, prodt_ref, dqt_ref, dk_ref, dv_ref,
):
    me = me_ref[0]
    group = q_ref.shape[0]
    blocks = group // rows
    reach = window // rows
    pairs = width // LANES
    scale = 1.0 / math.sqrt(HEAD_DIM)
    for blk in range(blocks):
        here = slice(blk * rows, (blk + 1) * rows)
        kt_ref[:, here] = k_ref[here, :].astype(f32).T.astype(bf16)
    dk_ref[...] = jnp.zeros_like(dk_ref)
    dv_ref[...] = jnp.zeros_like(dv_ref)

    def turn_back(grad, here):
        return (grad * cos_ref[here, :] - swap_halves(grad) * sin_ref[here, :]).astype(bf16)

    for blk in range(blocks):
        low = max(0, blk - reach)
        span = (blk + 1 - low) * rows
        slot = pl.multiple_of((me ^ blk) * rows, rows)
        here = slice(blk * rows, (blk + 1) * rows)
        fill_bias(bias_ref, begin_ref, blk, low, rows)
        prodt_ref[...] = (
            do_ref[pl.ds(slot, rows), :].astype(f32) * o_ref[pl.ds(slot, rows), :].astype(f32)
        ).T
        for head in range(2 * pairs):
            pair = head // 2
            cols = slice(pair * LANES, (pair + 1) * LANES)
            mine = slice(head * HEAD_DIM, (head + 1) * HEAD_DIM)
            query = head_mask(q_ref[here, cols], head % 2) * jnp.asarray(scale, bf16)
            grad = head_mask(do_ref[pl.ds(slot, rows), cols], head % 2)
            delta = jnp.sum(prodt_ref[mine, :], axis=0, keepdims=True)
            lse = lse_ref[head : head + 1, here]
            for at in range(0, span, CHUNK):
                keys = slice(low * rows + at, low * rows + at + CHUNK)
                score = dot_nt(k_ref[keys, cols], query) + bias_ref[at : at + CHUNK, :]
                prob = jnp.exp(score - lse)
                dprob = dot_nt(v_ref[keys, cols], grad)
                prob_ref[at : at + CHUNK, :] = prob.astype(bf16)
                ds_ref[at : at + CHUNK, :] = (prob * (dprob - delta)).astype(bf16)
            reachable = slice(low * rows, low * rows + span)
            dv_ref[reachable, cols] += dot_nn(prob_ref[:span, :], grad)
            dk_ref[reachable, cols] += dot_nn(ds_ref[:span, :], query)
            dqt_ref[mine, :] = dot_nn(kt_ref[mine, reachable], ds_ref[:span, :]) * scale
        dquery = dqt_ref[...].T
        for pair in range(pairs):
            cols = slice(pair * LANES, (pair + 1) * LANES)
            dlin_ref[pl.ds(slot, rows), cols] = turn_back(dquery[:, cols], here)
    for blk in range(blocks):
        slot = pl.multiple_of((me ^ blk) * rows, rows)
        here = slice(blk * rows, (blk + 1) * rows)
        for pair in range(pairs):
            cols = slice(pair * LANES, (pair + 1) * LANES)
            keycols = slice(width + pair * LANES, width + (pair + 1) * LANES)
            dlin_ref[pl.ds(slot, rows), keycols] = turn_back(dk_ref[here, cols], here)
        dlin_ref[pl.ds(slot, rows), 2 * width :] = dv_ref[here, :].astype(bf16)


def attend_forward(lin, tables, me, rows, width, window):
    group = lin.shape[0]
    heads = width // HEAD_DIM
    whole = pl.BlockSpec(memory_space=pltpu.VMEM)
    span = min(group, window + rows)
    return pl.pallas_call(
        functools.partial(forward_kernel, rows, width, window),
        out_shape=(
            jax.ShapeDtypeStruct((group, width), bf16),
            jax.ShapeDtypeStruct((group, width), bf16),
            jax.ShapeDtypeStruct((group, width), bf16),
            jax.ShapeDtypeStruct((group, width), bf16),
            jax.ShapeDtypeStruct((heads, group), f32),
        ),
        in_specs=[pl.BlockSpec(memory_space=pltpu.SMEM)] + [whole] * 4,
        out_specs=(whole,) * 5,
        scratch_shapes=[
            pltpu.VMEM((width, group), bf16),
            pltpu.VMEM((span, rows), f32),
            pltpu.VMEM((span, rows), f32),
            pltpu.VMEM((span, rows), bf16),
            pltpu.VMEM((width, rows), f32),
        ],
        compiler_params=pltpu.CompilerParams(vmem_limit_bytes=48 * 1024 * 1024),
        name="attend_forward",
    )(me, lin, *tables)


def attend_backward(grad, mixed, saved, tables, me, rows, width, window):
    query, keys, values, lse = saved
    group = query.shape[0]
    whole = pl.BlockSpec(memory_space=pltpu.VMEM)
    span = min(group, window + rows)
    return pl.pallas_call(
        functools.partial(backward_kernel, rows, width, window),
        out_shape=jax.ShapeDtypeStruct((group, 3 * width), bf16),
        in_specs=[pl.BlockSpec(memory_space=pltpu.SMEM)] + [whole] * 9,
        out_specs=whole,
        scratch_shapes=[
            pltpu.VMEM((width, group), bf16),
            pltpu.VMEM((span, rows), f32),
            pltpu.VMEM((span, rows), bf16),
            pltpu.VMEM((span, rows), bf16),
            pltpu.VMEM((width, rows), f32),
            pltpu.VMEM((width, rows), f32),
            pltpu.VMEM((group, width), f32),
            pltpu.VMEM((group, width), f32),
        ],
        compiler_params=pltpu.CompilerParams(vmem_limit_bytes=48 * 1024 * 1024),
        name="attend_backward",
    )(me, grad, mixed, query, keys, values, lse, *tables)


def position_tables(seq_lengths, group):
    row_ids = jnp.arange(group, dtype=jnp.int32)
    ends = jnp.cumsum(seq_lengths)
    starts = ends - seq_lengths
    begins = jnp.max(jnp.where(starts[None, :] <= row_ids[:, None], starts[None, :], 0), axis=1)
    place = (row_ids - begins).astype(f32)
    half = ROT_DIM // 2
    frequency = jnp.exp(jnp.arange(half, dtype=f32) * (-2.0 * math.log(10000.0) / ROT_DIM))
    lane = jnp.arange(LANES, dtype=jnp.int32) % HEAD_DIM
    lane_freq = jnp.where(lane < ROT_DIM, frequency[lane % half], 0.0)
    sign = jnp.where(lane < half, -1.0, 1.0).astype(f32)
    angle = place[:, None] * lane_freq[None, :]
    return jnp.cos(angle), jnp.sin(angle) * sign[None, :], begins[None, :].astype(jnp.int32)


def swap_mp(array, offset):
    count = lax.axis_size("mp")
    return lax.ppermute(array, "mp", [(i, i ^ offset) for i in range(count)])


def swap_dp(array, offset):
    count = lax.axis_size("dp")
    return lax.ppermute(array, "dp", [(i, i ^ offset) for i in range(count)])


def gather_pieces(piece):
    count = lax.axis_size("mp")
    pieces = [None] * count
    for chip in range(0, count, 2):
        pieces[chip] = piece if chip == 0 else swap_mp(piece, chip)
        pieces[chip + 1] = swap_mp(pieces[chip], 1)
    return pieces


def absolute_order(pieces, me):
    bit = 1
    while bit < len(pieces):
        flip = (me & bit) != 0
        pieces = [
            jnp.where(flip, pieces[i ^ bit], pieces[i]) for i in range(len(pieces))
        ]
        bit *= 2
    return pieces


def scatter_pieces(parts):
    count = lax.axis_size("mp")
    total = None
    for chip in list(range(2, count, 2)) + [0]:
        other = swap_mp(parts[chip + 1].astype(bf16), 1)
        both = parts[chip].astype(f32) + other.astype(f32)
        if chip:
            both = swap_mp(both.astype(bf16), chip).astype(f32)
        total = both if total is None else total + both
    return total


def scatter_dp(grad):
    count = lax.axis_size("dp")
    place = lax.axis_index("dp")
    bits = count.bit_length() - 1
    cols = grad.shape[1]
    now = grad.reshape((2,) * bits + (grad.shape[0] // count, cols))
    for bit in range(bits):
        axis = now.ndim - 3
        mine = (place >> bit) & 1
        keep = lax.dynamic_index_in_dim(now, mine, axis, keepdims=False)
        send = lax.dynamic_index_in_dim(now, 1 - mine, axis, keepdims=False)
        came = swap_dp(send, 1 << bit)
        now = keep.astype(f32) + came.astype(f32)
        if bit + 1 < bits:
            now = now.astype(bf16)
    return now


def sum_all(mp_first, rest):
    count = lax.axis_size("mp")
    step = 1
    while step < count:
        mp_first = mp_first + swap_mp(mp_first, step)
        step *= 2
    both = jnp.concatenate([mp_first, rest], axis=0)
    count = lax.axis_size("dp")
    step = 1
    while step < count:
        both = both + swap_dp(both, step)
        step *= 2
    return both


def gelu_pair(pre):
    cdf = 0.5 * (1.0 + lax.erf(pre * (1.0 / math.sqrt(2.0))))
    density = jnp.exp(-0.5 * pre * pre) * (1.0 / math.sqrt(2.0 * math.pi))
    return (pre * cdf).astype(bf16), (cdf + pre * density).astype(bf16)


def shards(
    hidden_in, cotangent, lengths, ln_gain, ln_bias, qkv_weight, qkv_bias,
    out_weight, out_bias, fc_weight, fc_bias, proj_weight, proj_bias,
):
    count = lax.axis_size("mp")
    me = lax.axis_index("mp")
    rows, model = hidden_in.shape
    group = rows * count
    width = model // count
    window = group // 2
    me_vec = me.astype(jnp.int32).reshape(1)
    tables = position_tables(lengths[0], group)
    gain = ln_gain.astype(f32)
    shift = ln_bias.astype(f32)

    def own_cols(array, axis):
        return jnp.concatenate(
            [
                lax.dynamic_slice_in_dim(array, part * model + me * width, width, axis)
                for part in range(3)
            ],
            axis=axis,
        )

    wqkv = [own_cols(qkv_weight[l], 1) for l in range(LAYERS)]
    bqkv = [own_cols(qkv_bias[l], 0).astype(f32) for l in range(LAYERS)]
    wout_own = [lax.dynamic_slice_in_dim(out_weight[l], me * width, width, 0) for l in range(LAYERS)]
    wout_rel = [
        jnp.concatenate(
            [
                lax.dynamic_slice_in_dim(out_weight[l], (me ^ k) * width, width, 0)
                for k in range(count)
            ],
            axis=0,
        )
        for l in range(LAYERS)
    ]
    pair_rows = 2 * rows

    hidden = hidden_in
    saved = []
    stat_rows = []
    for l in range(LAYERS):
        center, rstd = norm_stats(hidden)
        act = (center * rstd * gain[l] + shift[l]).astype(bf16)
        pieces = gather_pieces(act)
        near = jnp.concatenate(pieces[:2], axis=0)
        far = jnp.concatenate(pieces[2:], axis=0)
        acts = jnp.concatenate([near, far], axis=0)
        halves = []
        for part in (near, far):
            pre = dot_nn(part, fc_weight[l]) + fc_bias[l].astype(f32)
            halves.append(gelu_pair(pre))
        gelu = [h[0] for h in halves]
        slope = [h[1] for h in halves]
        far_out = dot_nt(gelu[1], proj_weight[l]).astype(bf16)
        near_out = dot_nt(gelu[0], proj_weight[l]).astype(bf16)
        outs = [near_out[:rows], near_out[rows:]] + [
            far_out[i * rows : (i + 1) * rows] for i in range(count - 2)
        ]
        ffn = scatter_pieces(outs) + proj_bias[l].astype(f32)
        lin = dot_nn(acts, wqkv[l]) + bqkv[l]
        mixed, query, keys, values, lse = attend_forward(
            lin, tables, me_vec, rows, width, window
        )
        mix_near = mixed[:pair_rows]
        got = {0: mix_near, 1: swap_mp(mix_near, 1)}
        for chip in range(2, count, 2):
            got[chip] = swap_mp(mixed[chip * rows : (chip + 2) * rows], chip)
            got[chip + 1] = swap_mp(got[chip], 1)
        own = [
            got[k][:rows] if k % 2 == 0 else got[k][rows:] for k in range(count)
        ]
        attn = dot_nn(jnp.concatenate(own, axis=1), wout_rel[l]) + out_bias[l].astype(f32)
        columns = []
        for k in range(0, count, 2):
            if k == 0:
                columns += [mixed, swap_mp(mixed[pair_rows:], 1)]
                continue
            order = [mixed[(s ^ k) * rows : (s ^ k) * rows + 2 * rows] for s in range(2, count, 2)]
            rest = swap_mp(jnp.concatenate(order, axis=0), k)
            columns += [jnp.concatenate([got[k], rest], axis=0), swap_mp(rest, 1)]
        full = []
        for k in range(count):
            if k % 2 == 0:
                full.append(columns[k])
                continue
            tail = columns[k]
            flipped = [got[k][rows:], got[k][:rows]]
            for s in range(0, count - 2, 2):
                flipped += [tail[(s + 1) * rows : (s + 2) * rows], tail[s * rows : (s + 1) * rows]]
            full.append(jnp.concatenate(flipped, axis=0))
        mixed_all = jnp.concatenate(full, axis=1)
        stat_rows.append(
            jnp.stack([jnp.sum(hidden * hidden), jnp.sum(attn * attn), jnp.sum(ffn * ffn)])
        )
        saved.append((hidden, acts, mixed, (query, keys, values, lse), mixed_all, gelu, slope))
        hidden = hidden + attn + ffn

    grad_res = cotangent
    out_grads = {}
    small = [None] * LAYERS
    for l in reversed(range(LAYERS)):
        hidden_l, acts, mixed, heads, mixed_all, gelu, slope = saved[l]
        branch = grad_res.astype(bf16)
        pieces = gather_pieces(branch)
        near = jnp.concatenate(pieces[:2], axis=0)
        far = jnp.concatenate(pieces[2:], axis=0)
        cots = jnp.concatenate([near, far], axis=0)
        dpre = [
            (dot_nn(part, proj_weight[l]) * slope[i].astype(f32)).astype(bf16)
            for i, part in enumerate((near, far))
        ]
        dmix = dot_nt(cots, wout_own[l]).astype(bf16)
        proj_grad = (dot_tn(near, gelu[0]) + dot_tn(far, gelu[1])).astype(bf16)
        out_grads["proj", l] = scatter_dp(proj_grad)
        own_cots = jnp.concatenate(
            [lax.dynamic_slice_in_dim(p, me * width, width, 1) for p in pieces], axis=0
        )
        out_rel = dot_tn(mixed_all, own_cots).astype(bf16)
        out_abs = jnp.concatenate(
            absolute_order([out_rel[k * width : (k + 1) * width] for k in range(count)], me), axis=0
        )
        dlin = attend_backward(dmix, mixed, heads, tables, me_vec, rows, width, window)
        fc_grad = (
            dot_tn(acts[:pair_rows], dpre[0]) + dot_tn(acts[pair_rows:], dpre[1])
        ).astype(bf16)
        out_grads["fc", l] = scatter_dp(fc_grad)
        qkv_grad = dot_tn(acts, dlin).astype(bf16)
        out_grads["att", l] = scatter_dp(jnp.concatenate([qkv_grad, out_abs], axis=1))
        far_da = (dot_nt(dpre[1], fc_weight[l]) + dot_nt(dlin[pair_rows:], wqkv[l])).astype(bf16)
        near_da = (dot_nt(dpre[0], fc_weight[l]) + dot_nt(dlin[:pair_rows], wqkv[l])).astype(bf16)
        parts = [near_da[:rows], near_da[rows:]] + [
            far_da[i * rows : (i + 1) * rows] for i in range(count - 2)
        ]
        dact = scatter_pieces(parts)
        center, rstd = norm_stats(hidden_l)
        normed = center * rstd
        dnormed = dact * gain[l]
        dhidden = rstd * (
            dnormed
            - jnp.mean(dnormed, axis=-1, keepdims=True)
            - normed * jnp.mean(dnormed * normed, axis=-1, keepdims=True)
        )
        qkvb = jnp.sum(dlin.astype(f32), axis=0).reshape(3, width)
        qkvb_rows = lax.dynamic_update_slice_in_dim(
            jnp.zeros((3, model), f32), qkvb, me * width, 1
        )
        fcb = sum(jnp.sum(d.astype(f32), axis=0) for d in dpre)
        stats_row = jnp.pad(stat_rows[l], (0, model - 3))
        mine = jnp.concatenate(
            [
                jnp.sum(dact * normed, axis=0)[None],
                jnp.sum(dact, axis=0)[None],
                jnp.sum(branch.astype(f32), axis=0)[None],
                qkvb_rows,
                stats_row[None],
            ],
            axis=0,
        )
        small[l] = sum_all(mine, jnp.pad(fcb, (0, -fcb.shape[0] % model)).reshape(-1, model))
        grad_res = grad_res + dhidden

    qkv_total, outw_total = [], []
    for l in range(LAYERS):
        pieces = absolute_order(gather_pieces(out_grads["att", l].astype(bf16)), me)
        qkv_total.append(
            jnp.concatenate(
                [p[:, part * width : (part + 1) * width] for part in range(3) for p in pieces],
                axis=1,
            ).astype(f32)
        )
        outw_total.append(jnp.concatenate([p[:, 3 * width :] for p in pieces], axis=1).astype(f32))
    entries = float(rows * lax.axis_size("dp") * count * model)
    outb = jnp.stack([s[2] for s in small])
    return (
        hidden,
        grad_res,
        jnp.sqrt(jnp.stack([s[6, :3] for s in small]) / entries),
        jnp.stack([s[0] for s in small]),
        jnp.stack([s[1] for s in small]),
        jnp.stack(qkv_total),
        jnp.stack([s[3:6].reshape(-1) for s in small]),
        jnp.stack(outw_total),
        outb,
        jnp.stack([out_grads["fc", l] for l in range(LAYERS)]),
        jnp.stack([s[7:].reshape(-1)[: fc_bias.shape[1]] for s in small]),
        jnp.stack([out_grads["proj", l] for l in range(LAYERS)]),
        outb,
    )


def solution(mesh):
    tokens = P(("dp", "mp"), None)
    hidden_units = P(None, None, "mp")
    return jax.shard_map(
        shards,
        mesh=mesh,
        in_specs=(
            tokens, tokens, P("dp", None), P(), P(), P(), P(), P(), P(),
            hidden_units, P(None, "mp"), hidden_units, P(),
        ),
        out_specs=(
            tokens, tokens, P(), P(), P(), P(None, "dp", None), P(), P(None, "dp", None), P(),
            P(None, "dp", "mp"), P(None, "mp"), P(None, "dp", "mp"), P(),
        ),
        check_vma=False,
    )
```

```python
import functools
import math

import jax
import jax.numpy as jnp
from jax import lax
from jax.experimental import pallas as pl
from jax.experimental.pallas import tpu as pltpu
from jax.sharding import PartitionSpec as P

HEADS = 16
HEAD_DIM = 64
ROT_DIM = 16
LAYERS = 2

EPS = 1e-05
NEG = -1e30
LANES = 128
CHUNK = 128


f32 = jnp.float32
bf16 = jnp.bfloat16


def norm_stats(hidden):
    center = hidden - jnp.mean(hidden, axis=-1, keepdims=True)
    spread = jnp.mean(center * center, axis=-1, keepdims=True)
    return center, lax.rsqrt(spread + EPS)


def dot_nn(left, right):
    return lax.dot_general(left, right, (((1,), (0,)), ((), ())), preferred_element_type=f32)


def dot_nt(left, right):
    return lax.dot_general(left, right, (((1,), (1,)), ((), ())), preferred_element_type=f32)


def dot_tn(left, right):
    return lax.dot_general(left, right, (((0,), (0,)), ((), ())), preferred_element_type=f32)


def swap_halves(block):
    lane = lax.broadcasted_iota(jnp.int32, block.shape, 1) % HEAD_DIM
    half = ROT_DIM // 2
    return jnp.where(
        lane < half, pltpu.roll(block, LANES - half, 1), pltpu.roll(block, half, 1)
    )


def head_mask(block, which):
    lane = lax.broadcasted_iota(jnp.int32, block.shape, 1)
    keep = (lane < HEAD_DIM) if which == 0 else (lane >= HEAD_DIM)
    return jnp.where(keep, block, jnp.zeros_like(block))


def fill_bias(bias_ref, begin_ref, blk, low, rows):
    begin = begin_ref[:, blk * rows : (blk + 1) * rows]
    query = blk * rows + lax.broadcasted_iota(jnp.int32, (CHUNK, rows), 1)
    for start in range(low * rows, (blk + 1) * rows, CHUNK):
        key = start + lax.broadcasted_iota(jnp.int32, (CHUNK, rows), 0)
        keep = (key >= begin) & (key <= query)
        bias_ref[start - low * rows : start - low * rows + CHUNK, :] = jnp.where(keep, 0.0, NEG)


def forward_kernel(
    rows, width, window, me_ref, lin_ref, cos_ref, sin_ref, begin_ref,
    out_ref, q_ref, k_ref, v_ref, lse_ref,
    vt_ref, bias_ref, score_ref, prob_ref, ot_ref,
):
    me = me_ref[0]
    group = q_ref.shape[0]
    blocks = group // rows
    reach = window // rows
    pairs = width // LANES
    scale = 1.0 / math.sqrt(HEAD_DIM)
    for blk in range(blocks):
        slot = pl.multiple_of((me ^ blk) * rows, rows)
        here = slice(blk * rows, (blk + 1) * rows)
        cosine, sine = cos_ref[here, :], sin_ref[here, :]
        for part, ref in ((0, q_ref), (1, k_ref)):
            for pair in range(pairs):
                cols = slice(part * width + pair * LANES, part * width + (pair + 1) * LANES)
                block = lin_ref[pl.ds(slot, rows), cols]
                turned = block * cosine + swap_halves(block) * sine
                ref[here, pair * LANES : (pair + 1) * LANES] = turned.astype(bf16)
        value = lin_ref[pl.ds(slot, rows), 2 * width :]
        v_ref[here, :] = value.astype(bf16)
        vt_ref[:, here] = value.T.astype(bf16)
    for blk in range(blocks):
        low = max(0, blk - reach)
        span = (blk + 1 - low) * rows
        slot = pl.multiple_of((me ^ blk) * rows, rows)
        here = slice(blk * rows, (blk + 1) * rows)
        fill_bias(bias_ref, begin_ref, blk, low, rows)
        for head in range(2 * pairs):
            pair = head // 2
            cols = slice(pair * LANES, (pair + 1) * LANES)
            query = head_mask(q_ref[here, cols], head % 2) * jnp.asarray(scale, bf16)
            best = jnp.full((1, rows), NEG, f32)
            for at in range(0, span, CHUNK):
                keys = k_ref[low * rows + at : low * rows + at + CHUNK, cols]
                score = dot_nt(keys, query) + bias_ref[at : at + CHUNK, :]
                score_ref[at : at + CHUNK, :] = score
                best = jnp.maximum(best, jnp.max(score, axis=0, keepdims=True))
            total = jnp.zeros((1, rows), f32)
            for at in range(0, span, CHUNK):
                weight = jnp.exp(score_ref[at : at + CHUNK, :] - best)
                total = total + jnp.sum(weight, axis=0, keepdims=True)
                prob_ref[at : at + CHUNK, :] = weight.astype(bf16)
            mixed = dot_nn(
                vt_ref[head * HEAD_DIM : (head + 1) * HEAD_DIM, low * rows : low * rows + span],
                prob_ref[:span, :],
            )
            ot_ref[head * HEAD_DIM : (head + 1) * HEAD_DIM, :] = mixed * (1.0 / total)
            lse_ref[head : head + 1, here] = best + jnp.log(total)
        out_ref[pl.ds(slot, rows), :] = ot_ref[...].T.astype(bf16)


def backward_kernel(
    rows, width, window, me_ref, do_ref, o_ref, q_ref, k_ref, v_ref, lse_ref,
    cos_ref, sin_ref, begin_ref, dlin_ref,
    kt_ref, bias_ref, prob_ref, ds_ref, prodt_ref, dqt_ref, dk_ref, dv_ref,
):
    me = me_ref[0]
    group = q_ref.shape[0]
    blocks = group // rows
    reach = window // rows
    pairs = width // LANES
    scale = 1.0 / math.sqrt(HEAD_DIM)
    for blk in range(blocks):
        here = slice(blk * rows, (blk + 1) * rows)
        kt_ref[:, here] = k_ref[here, :].astype(f32).T.astype(bf16)
    dk_ref[...] = jnp.zeros_like(dk_ref)
    dv_ref[...] = jnp.zeros_like(dv_ref)

    def turn_back(grad, here):
        return (grad * cos_ref[here, :] - swap_halves(grad) * sin_ref[here, :]).astype(bf16)

    for blk in range(blocks):
        low = max(0, blk - reach)
        span = (blk + 1 - low) * rows
        slot = pl.multiple_of((me ^ blk) * rows, rows)
        here = slice(blk * rows, (blk + 1) * rows)
        fill_bias(bias_ref, begin_ref, blk, low, rows)
        prodt_ref[...] = (
            do_ref[pl.ds(slot, rows), :].astype(f32) * o_ref[pl.ds(slot, rows), :].astype(f32)
        ).T
        for head in range(2 * pairs):
            pair = head // 2
            cols = slice(pair * LANES, (pair + 1) * LANES)
            mine = slice(head * HEAD_DIM, (head + 1) * HEAD_DIM)
            query = head_mask(q_ref[here, cols], head % 2) * jnp.asarray(scale, bf16)
            grad = head_mask(do_ref[pl.ds(slot, rows), cols], head % 2)
            delta = jnp.sum(prodt_ref[mine, :], axis=0, keepdims=True)
            lse = lse_ref[head : head + 1, here]
            for at in range(0, span, CHUNK):
                keys = slice(low * rows + at, low * rows + at + CHUNK)
                score = dot_nt(k_ref[keys, cols], query) + bias_ref[at : at + CHUNK, :]
                prob = jnp.exp(score - lse)
                dprob = dot_nt(v_ref[keys, cols], grad)
                prob_ref[at : at + CHUNK, :] = prob.astype(bf16)
                ds_ref[at : at + CHUNK, :] = (prob * (dprob - delta)).astype(bf16)
            reachable = slice(low * rows, low * rows + span)
            dv_ref[reachable, cols] += dot_nn(prob_ref[:span, :], grad)
            dk_ref[reachable, cols] += dot_nn(ds_ref[:span, :], query)
            dqt_ref[mine, :] = dot_nn(kt_ref[mine, reachable], ds_ref[:span, :]) * scale
        dquery = dqt_ref[...].T
        for pair in range(pairs):
            cols = slice(pair * LANES, (pair + 1) * LANES)
            dlin_ref[pl.ds(slot, rows), cols] = turn_back(dquery[:, cols], here)
    for blk in range(blocks):
        slot = pl.multiple_of((me ^ blk) * rows, rows)
        here = slice(blk * rows, (blk + 1) * rows)
        for pair in range(pairs):
            cols = slice(pair * LANES, (pair + 1) * LANES)
            keycols = slice(width + pair * LANES, width + (pair + 1) * LANES)
            dlin_ref[pl.ds(slot, rows), keycols] = turn_back(dk_ref[here, cols], here)
        dlin_ref[pl.ds(slot, rows), 2 * width :] = dv_ref[here, :].astype(bf16)


def attend_forward(lin, tables, me, rows, width, window):
    group = lin.shape[0]
    heads = width // HEAD_DIM
    whole = pl.BlockSpec(memory_space=pltpu.VMEM)
    span = min(group, window + rows)
    return pl.pallas_call(
        functools.partial(forward_kernel, rows, width, window),
        out_shape=(
            jax.ShapeDtypeStruct((group, width), bf16),
            jax.ShapeDtypeStruct((group, width), bf16),
            jax.ShapeDtypeStruct((group, width), bf16),
            jax.ShapeDtypeStruct((group, width), bf16),
            jax.ShapeDtypeStruct((heads, group), f32),
        ),
        in_specs=[pl.BlockSpec(memory_space=pltpu.SMEM)] + [whole] * 4,
        out_specs=(whole,) * 5,
        scratch_shapes=[
            pltpu.VMEM((width, group), bf16),
            pltpu.VMEM((span, rows), f32),
            pltpu.VMEM((span, rows), f32),
            pltpu.VMEM((span, rows), bf16),
            pltpu.VMEM((width, rows), f32),
        ],
        compiler_params=pltpu.CompilerParams(vmem_limit_bytes=48 * 1024 * 1024),
        name="attend_forward",
    )(me, lin, *tables)


def attend_backward(grad, mixed, saved, tables, me, rows, width, window):
    query, keys, values, lse = saved
    group = query.shape[0]
    whole = pl.BlockSpec(memory_space=pltpu.VMEM)
    span = min(group, window + rows)
    return pl.pallas_call(
        functools.partial(backward_kernel, rows, width, window),
        out_shape=jax.ShapeDtypeStruct((group, 3 * width), bf16),
        in_specs=[pl.BlockSpec(memory_space=pltpu.SMEM)] + [whole] * 9,
        out_specs=whole,
        scratch_shapes=[
            pltpu.VMEM((width, group), bf16),
            pltpu.VMEM((span, rows), f32),
            pltpu.VMEM((span, rows), bf16),
            pltpu.VMEM((span, rows), bf16),
            pltpu.VMEM((width, rows), f32),
            pltpu.VMEM((width, rows), f32),
            pltpu.VMEM((group, width), f32),
            pltpu.VMEM((group, width), f32),
        ],
        compiler_params=pltpu.CompilerParams(vmem_limit_bytes=48 * 1024 * 1024),
        name="attend_backward",
    )(me, grad, mixed, query, keys, values, lse, *tables)


def position_tables(seq_lengths, group):
    row_ids = jnp.arange(group, dtype=jnp.int32)
    ends = jnp.cumsum(seq_lengths)
    starts = ends - seq_lengths
    begins = jnp.max(jnp.where(starts[None, :] <= row_ids[:, None], starts[None, :], 0), axis=1)
    place = (row_ids - begins).astype(f32)
    half = ROT_DIM // 2
    lane = jnp.arange(LANES, dtype=jnp.int32) % HEAD_DIM
    frequency = jnp.exp((lane % half).astype(f32) * (-2.0 * math.log(10000.0) / ROT_DIM))
    lane_freq = jnp.where(lane < ROT_DIM, frequency, 0.0)
    sign = jnp.where(lane < half, -1.0, 1.0).astype(f32)
    angle = place[:, None] * lane_freq[None, :]
    return jnp.cos(angle), jnp.sin(angle) * sign[None, :], begins[None, :].astype(jnp.int32)


def swap_mp(array, offset):
    count = lax.axis_size("mp")
    return lax.ppermute(array, "mp", [(i, i ^ offset) for i in range(count)])


def swap_dp(array, offset):
    count = lax.axis_size("dp")
    return lax.ppermute(array, "dp", [(i, i ^ offset) for i in range(count)])


def tie(array, *after):
    return lax.optimization_barrier((array,) + after)[0]


def gather_pieces(piece):
    count = lax.axis_size("mp")
    pieces = [None] * count
    for chip in range(0, count, 2):
        pieces[chip] = piece if chip == 0 else swap_mp(piece, chip)
        pieces[chip + 1] = swap_mp(pieces[chip], 1)
    return pieces


def absolute_order(pieces, me):
    bit = 1
    while bit < len(pieces):
        flip = (me & bit) != 0
        pieces = [
            jnp.where(flip, pieces[i ^ bit], pieces[i]) for i in range(len(pieces))
        ]
        bit *= 2
    return pieces


def chip_sums(parts, chips):
    return {
        chip: parts[chip].astype(f32) + swap_mp(parts[chip + 1].astype(bf16), 1).astype(f32)
        for chip in chips
    }


class DpScatter:

    def __init__(self, grad):
        count = lax.axis_size("dp")
        self.bits = count.bit_length() - 1
        self.bit = 0
        self.now = grad.reshape(count, grad.shape[0] // count, grad.shape[1])
        self.send()

    def send(self):
        upper = ((lax.axis_index("dp") >> self.bit) & 1) != 0
        pairs = self.now.reshape((-1, 2) + self.now.shape[1:])
        self.keep = jnp.where(upper, pairs[:, 1], pairs[:, 0])
        self.came = swap_dp(jnp.where(upper, pairs[:, 0], pairs[:, 1]), 1 << self.bit)

    def step(self, *after):
        if self.bit == self.bits:
            return
        came = tie(self.came, *after) if after else self.came
        self.now = self.keep.astype(f32) + came.astype(f32)
        self.bit += 1
        if self.bit < self.bits:
            self.now = self.now.astype(bf16)
            self.send()

    def total(self):
        while self.bit < self.bits:
            self.step()
        return self.now[0]


def sum_all(mp_first, rest):
    count = lax.axis_size("mp")
    step = 1
    while step < count:
        mp_first = mp_first + swap_mp(mp_first, step)
        step *= 2
    both = jnp.concatenate([mp_first, rest], axis=0)
    count = lax.axis_size("dp")
    step = 1
    while step < count:
        both = both + swap_dp(both, step)
        step *= 2
    return both


def gelu_pair(pre):
    cdf = 0.5 * (1.0 + lax.erf(pre * (1.0 / math.sqrt(2.0))))
    density = jnp.exp(-0.5 * pre * pre) * (1.0 / math.sqrt(2.0 * math.pi))
    return (pre * cdf).astype(bf16), (cdf + pre * density).astype(bf16)


def shards(
    hidden_in, cotangent, lengths, ln_gain, ln_bias, qkv_weight, qkv_bias,
    out_weight, out_bias, fc_weight, fc_bias, proj_weight, proj_bias,
):
    count = lax.axis_size("mp")
    me = lax.axis_index("mp")
    rows, model = hidden_in.shape
    group = rows * count
    width = model // count
    window = group // 2
    me_vec = me.astype(jnp.int32).reshape(1)
    tables = position_tables(lengths[0], group)
    gain = ln_gain.astype(f32)
    shift = ln_bias.astype(f32)

    def layer_slice(array, layer, start, size):
        return lax.dynamic_slice(array, (layer,) + start, (1,) + size)[0]

    def own_cols(layer):
        return jnp.concatenate(
            [
                layer_slice(qkv_weight, layer, (0, part * model + me * width), (model, width))
                for part in range(3)
            ],
            axis=1,
        )

    def own_bias(layer):
        return jnp.concatenate(
            [
                layer_slice(qkv_bias, layer, (part * model + me * width,), (width,))
                for part in range(3)
            ]
        ).astype(f32)

    def out_rows(layer, k):
        return layer_slice(out_weight, layer, ((me ^ k) * width, 0), (width, model))

    wqkv = [own_cols(l) for l in range(LAYERS)]
    bqkv = [own_bias(l) for l in range(LAYERS)]
    wout_own = [out_rows(l, 0) for l in range(LAYERS)]
    wout_rel = [
        jnp.concatenate([out_rows(l, k) for k in range(count)], axis=0) for l in range(LAYERS)
    ]
    pair_rows = 2 * rows
    far_chips = range(2, count, 2)

    def split_rows(near, far):
        return [near[:rows], near[rows:]] + [
            far[i * rows : (i + 1) * rows] for i in range(count - 2)
        ]

    def fc_part(part, l):
        return gelu_pair(dot_nn(part, fc_weight[l]) + fc_bias[l].astype(f32))

    hidden = hidden_in
    saved = []
    stat_rows = []
    for l in range(LAYERS):
        center, rstd = norm_stats(hidden)
        act = (center * rstd * gain[l] + shift[l]).astype(bf16)
        away = {chip: swap_mp(act, chip) for chip in far_chips}
        near = jnp.concatenate([act, swap_mp(act, 1)], axis=0)
        gelu_near, slope_near = fc_part(near, l)
        pieces = []
        for chip in far_chips:
            arrived = tie(away[chip], gelu_near)
            pieces += [arrived, swap_mp(arrived, 1)]
        near_out = dot_nt(gelu_near, proj_weight[l]).astype(bf16)
        pieces[1] = tie(pieces[1], near_out)
        far = jnp.concatenate(pieces, axis=0)
        acts = jnp.concatenate([near, far], axis=0)
        gelu_far, slope_far = fc_part(far, l)
        far_out = dot_nt(gelu_far, proj_weight[l]).astype(bf16)
        outs = split_rows(near_out, far_out)
        sums = chip_sums(outs, far_chips)
        sending = {chip: sums[chip].astype(bf16) for chip in far_chips}
        returned = {chip: swap_mp(sending[chip], chip) for chip in far_chips}
        lin = dot_nn(tie(acts, *sending.values()), wqkv[l]) + bqkv[l]
        mixed, query, keys, values, lse = attend_forward(
            lin, tables, me_vec, rows, width, window
        )
        mix_near = mixed[:pair_rows]
        got = {0: mix_near, 1: swap_mp(mix_near, 1)}
        for chip in far_chips:
            got[chip] = swap_mp(mixed[chip * rows : (chip + 2) * rows], chip)
            got[chip + 1] = swap_mp(got[chip], 1)
        ffn = chip_sums(outs, [0])[0] + proj_bias[l].astype(f32)
        for chip in far_chips:
            ffn = ffn + tie(returned[chip], mixed).astype(f32)
        own = [got[k][:rows] if k % 2 == 0 else got[k][rows:] for k in range(count)]
        attn = dot_nn(jnp.concatenate(own, axis=1), wout_rel[l]) + out_bias[l].astype(f32)
        full = []
        for k in range(0, count, 2):
            if k == 0:
                rest = mixed[pair_rows:]
            else:
                order = [mixed[(s ^ k) * rows : (s ^ k) * rows + 2 * rows] for s in far_chips]
                rest = swap_mp(jnp.concatenate(order, axis=0), k)
            tail = swap_mp(rest, 1)
            flipped = [got[k + 1][rows:], got[k + 1][:rows]]
            for s in range(0, count - 2, 2):
                flipped += [tail[(s + 1) * rows : (s + 2) * rows], tail[s * rows : (s + 1) * rows]]
            full += [jnp.concatenate([got[k], rest], axis=0), jnp.concatenate(flipped, axis=0)]
        mixed_all = jnp.concatenate(full, axis=1)
        stat_rows.append(
            jnp.stack([jnp.sum(hidden * hidden), jnp.sum(attn * attn), jnp.sum(ffn * ffn)])
        )
        saved.append(
            (
                hidden, acts, mixed, (query, keys, values, lse), mixed_all,
                (gelu_near, gelu_far), (slope_near, slope_far),
            )
        )
        hidden = hidden + attn + ffn

    grad_res = cotangent
    grads = {}
    small_mp, small_dp = [None] * LAYERS, [None] * LAYERS

    def advance(layer, names, *after):
        if layer < LAYERS:
            for name in names:
                grads[name, layer].step(*after)

    for l in reversed(range(LAYERS)):
        hidden_l, acts, mixed, heads, mixed_all, gelu, slope = saved[l]
        branch = grad_res.astype(bf16)
        away = {chip: swap_mp(branch, chip) for chip in far_chips}
        near_pieces = [branch, swap_mp(branch, 1)]
        near = jnp.concatenate(near_pieces, axis=0)
        dpre_near = (dot_nn(near, proj_weight[l]) * slope[0].astype(f32)).astype(bf16)
        far_pieces = []
        for chip in far_chips:
            arrived = tie(away[chip], dpre_near)
            far_pieces += [arrived, swap_mp(arrived, 1)]
        far = jnp.concatenate(far_pieces, axis=0)
        cots = jnp.concatenate([near, far], axis=0)
        dmix = dot_nt(cots, wout_own[l]).astype(bf16)
        dpre_far = (dot_nn(far, proj_weight[l]) * slope[1].astype(f32)).astype(bf16)
        advance(l + 1, ["fc"], dpre_far)
        advance(l + 1, ["proj", "out"], dpre_far)
        proj_grad = (dot_tn(near, gelu[0]) + dot_tn(far, gelu[1])).astype(bf16)
        grads["proj", l] = DpScatter(proj_grad)
        dlin = attend_backward(dmix, mixed, heads, tables, me_vec, rows, width, window)
        advance(l + 1, ["qkv", "fc"], dlin)
        far_da = (dot_nt(dpre_far, fc_weight[l]) + dot_nt(dlin[pair_rows:], wqkv[l])).astype(bf16)
        sums = chip_sums([None, None] + split_rows(far_da, far_da)[2:], far_chips)
        sending = {chip: sums[chip].astype(bf16) for chip in far_chips}
        returned = {chip: swap_mp(sending[chip], chip) for chip in far_chips}
        acts_late, cots_late, dlin_late = lax.optimization_barrier(
            (acts, tuple(near_pieces + far_pieces), dlin) + tuple(sending.values())
        )[:3]
        near_da = (dot_nt(dpre_near, fc_weight[l]) + dot_nt(dlin_late[:pair_rows], wqkv[l])).astype(
            bf16
        )
        fc_grad = (
            dot_tn(acts_late[:pair_rows], dpre_near) + dot_tn(acts_late[pair_rows:], dpre_far)
        ).astype(bf16)
        grads["fc", l] = DpScatter(fc_grad)
        qkv_grad = dot_tn(acts_late, dlin_late).astype(bf16)
        grads["qkv", l] = DpScatter(qkv_grad)
        own_cots = jnp.concatenate(
            [lax.dynamic_slice_in_dim(p, me * width, width, 1) for p in cots_late], axis=0
        )
        out_rel = dot_tn(mixed_all, own_cots).astype(bf16)
        out_abs = jnp.concatenate(
            absolute_order([out_rel[k * width : (k + 1) * width] for k in range(count)], me), axis=0
        )
        grads["out", l] = DpScatter(out_abs)
        dact = chip_sums([near_da[:rows], near_da[rows:]], [0])[0]
        for chip in far_chips:
            dact = dact + tie(returned[chip], qkv_grad).astype(f32)
        advance(l, ["proj"], dact)
        advance(l + 1, ["proj", "out", "fc", "qkv"], dact)
        center, rstd = norm_stats(hidden_l)
        normed = center * rstd
        dnormed = dact * gain[l]
        dhidden = rstd * (
            dnormed
            - jnp.mean(dnormed, axis=-1, keepdims=True)
            - normed * jnp.mean(dnormed * normed, axis=-1, keepdims=True)
        )
        qkvb = jnp.sum(dlin.astype(f32), axis=0).reshape(3, width)
        qkvb_rows = lax.dynamic_update_slice_in_dim(
            jnp.zeros((3, model), f32), qkvb, me * width, 1
        )
        fcb = jnp.sum(dpre_near.astype(f32), axis=0) + jnp.sum(dpre_far.astype(f32), axis=0)
        stats_row = jnp.pad(stat_rows[l], (0, model - 3))
        small_mp[l] = jnp.concatenate(
            [
                jnp.sum(dact * normed, axis=0)[None],
                jnp.sum(dact, axis=0)[None],
                jnp.sum(branch.astype(f32), axis=0)[None],
                qkvb_rows,
                stats_row[None],
            ],
            axis=0,
        )
        small_dp[l] = jnp.pad(fcb, (0, -fcb.shape[0] % model)).reshape(-1, model)
        grad_res = grad_res + dhidden

    lines = small_mp[0].shape[0]
    sums = sum_all(jnp.concatenate(small_mp, axis=0), jnp.concatenate(small_dp, axis=0))
    small = [sums[l * lines : (l + 1) * lines] for l in range(LAYERS)]
    fcb_rows = sums[LAYERS * lines :].reshape(LAYERS, -1)
    qkv_total, outw_total = [], []
    for l in range(LAYERS):
        both = jnp.concatenate(
            [grads["qkv", l].total().astype(bf16), grads["out", l].total().astype(bf16)], axis=1
        )
        pieces = absolute_order(gather_pieces(both), me)
        qkv_total.append(
            jnp.concatenate(
                [p[:, part * width : (part + 1) * width] for part in range(3) for p in pieces],
                axis=1,
            ).astype(f32)
        )
        outw_total.append(jnp.concatenate([p[:, 3 * width :] for p in pieces], axis=1).astype(f32))
    entries = float(rows * lax.axis_size("dp") * count * model)
    outb = jnp.stack([s[2] for s in small])
    return (
        hidden,
        grad_res,
        jnp.sqrt(jnp.stack([s[6, :3] for s in small]) / entries),
        jnp.stack([s[0] for s in small]),
        jnp.stack([s[1] for s in small]),
        jnp.stack(qkv_total),
        jnp.stack([s[3:6].reshape(-1) for s in small]),
        jnp.stack(outw_total),
        outb,
        jnp.stack([grads["fc", l].total() for l in range(LAYERS)]),
        fcb_rows[:, : fc_bias.shape[1]],
        jnp.stack([grads["proj", l].total() for l in range(LAYERS)]),
        outb,
    )


def solution(mesh):
    tokens = P(("dp", "mp"), None)
    hidden_units = P(None, None, "mp")
    return jax.shard_map(
        shards,
        mesh=mesh,
        in_specs=(
            tokens, tokens, P("dp", None), P(), P(), P(), P(), P(), P(),
            hidden_units, P(None, "mp"), hidden_units, P(),
        ),
        out_specs=(
            tokens, tokens, P(), P(), P(), P(None, "dp", None), P(), P(None, "dp", None), P(),
            P(None, "dp", "mp"), P(None, "mp"), P(None, "dp", "mp"), P(),
        ),
        check_vma=False,
    )
```

```python
import functools
import math

import jax
import jax.numpy as jnp
from jax import lax
from jax.experimental import pallas as pl
from jax.experimental.pallas import tpu as pltpu
from jax.sharding import PartitionSpec as P


HEAD_DIM = 64
ROT_DIM = 16
LAYERS = 2

EPS = 1e-05
NEG = -1e30
LANES = 128
PROJ, FC, QKV, OUT = "pcqo"
CHUNK = 128


f32 = jnp.float32
bf16 = jnp.bfloat16


def norm_stats(hidden):
    center = hidden - jnp.mean(hidden, axis=-1, keepdims=True)
    spread = jnp.mean(center * center, axis=-1, keepdims=True)
    return center, lax.rsqrt(spread + EPS)


def dot_nn(left, right):
    return lax.dot_general(left, right, (((1,), (0,)), ((), ())), preferred_element_type=f32)


def dot_nt(left, right):
    return lax.dot_general(left, right, (((1,), (1,)), ((), ())), preferred_element_type=f32)


def dot_tn(left, right):
    return lax.dot_general(left, right, (((0,), (0,)), ((), ())), preferred_element_type=f32)


def swap_halves(block):
    lane = lax.broadcasted_iota(jnp.int32, block.shape, 1) % HEAD_DIM
    half = ROT_DIM // 2
    return jnp.where(
        lane < half, pltpu.roll(block, LANES - half, 1), pltpu.roll(block, half, 1)
    )


def head_mask(block, which):
    lane = lax.broadcasted_iota(jnp.int32, block.shape, 1)
    keep = (lane < HEAD_DIM) if which == 0 else (lane >= HEAD_DIM)
    return jnp.where(keep, block, jnp.zeros_like(block))


def fill_bias(bias_ref, begin_ref, blk, low, rows):
    begin = begin_ref[:, blk * rows : (blk + 1) * rows]
    query = blk * rows + lax.broadcasted_iota(jnp.int32, (CHUNK, rows), 1)
    for start in range(low * rows, (blk + 1) * rows, CHUNK):
        key = start + lax.broadcasted_iota(jnp.int32, (CHUNK, rows), 0)
        keep = (key >= begin) & (key <= query)
        bias_ref[start - low * rows : start - low * rows + CHUNK, :] = jnp.where(keep, 0.0, NEG)


def forward_kernel(
    rows, width, window, me_ref, lin_ref, cos_ref, sin_ref, begin_ref,
    out_ref, q_ref, k_ref, v_ref, lse_ref,
    vt_ref, bias_ref, score_ref, prob_ref, ot_ref,
):
    me = me_ref[0]
    group = q_ref.shape[0]
    blocks = group // rows
    reach = window // rows
    pairs = width // LANES
    scale = 1.0 / math.sqrt(HEAD_DIM)
    for blk in range(blocks):
        slot = pl.multiple_of((me ^ blk) * rows, rows)
        here = slice(blk * rows, (blk + 1) * rows)
        cosine, sine = cos_ref[here, :], sin_ref[here, :]
        for part, ref in ((0, q_ref), (1, k_ref)):
            for pair in range(pairs):
                cols = slice(part * width + pair * LANES, part * width + (pair + 1) * LANES)
                block = lin_ref[pl.ds(slot, rows), cols]
                turned = block * cosine + swap_halves(block) * sine
                ref[here, pair * LANES : (pair + 1) * LANES] = turned.astype(bf16)
        value = lin_ref[pl.ds(slot, rows), 2 * width :]
        v_ref[here, :] = value.astype(bf16)
        vt_ref[:, here] = value.T.astype(bf16)
    for blk in range(blocks):
        low = max(0, blk - reach)
        span = (blk + 1 - low) * rows
        slot = pl.multiple_of((me ^ blk) * rows, rows)
        here = slice(blk * rows, (blk + 1) * rows)
        fill_bias(bias_ref, begin_ref, blk, low, rows)
        for head in range(2 * pairs):
            pair = head // 2
            cols = slice(pair * LANES, (pair + 1) * LANES)
            query = head_mask(q_ref[here, cols], head % 2) * jnp.asarray(scale, bf16)
            best = jnp.full((1, rows), NEG, f32)
            for at in range(0, span, CHUNK):
                keys = k_ref[low * rows + at : low * rows + at + CHUNK, cols]
                score = dot_nt(keys, query) + bias_ref[at : at + CHUNK, :]
                score_ref[at : at + CHUNK, :] = score
                best = jnp.maximum(best, jnp.max(score, axis=0, keepdims=True))
            total = jnp.zeros((1, rows), f32)
            for at in range(0, span, CHUNK):
                weight = jnp.exp(score_ref[at : at + CHUNK, :] - best)
                total = total + jnp.sum(weight, axis=0, keepdims=True)
                prob_ref[at : at + CHUNK, :] = weight.astype(bf16)
            mixed = dot_nn(
                vt_ref[head * HEAD_DIM : (head + 1) * HEAD_DIM, low * rows : low * rows + span],
                prob_ref[:span, :],
            )
            ot_ref[head * HEAD_DIM : (head + 1) * HEAD_DIM, :] = mixed * (1.0 / total)
            lse_ref[head : head + 1, here] = best + jnp.log(total)
        out_ref[pl.ds(slot, rows), :] = ot_ref[...].T.astype(bf16)


def backward_kernel(
    rows, width, window, me_ref, do_ref, o_ref, q_ref, k_ref, v_ref, lse_ref,
    cos_ref, sin_ref, begin_ref, dlin_ref,
    kt_ref, bias_ref, prob_ref, ds_ref, prodt_ref, dqt_ref, dk_ref, dv_ref,
):
    me = me_ref[0]
    group = q_ref.shape[0]
    blocks = group // rows
    reach = window // rows
    pairs = width // LANES
    scale = 1.0 / math.sqrt(HEAD_DIM)
    for blk in range(blocks):
        here = slice(blk * rows, (blk + 1) * rows)
        kt_ref[:, here] = k_ref[here, :].astype(f32).T.astype(bf16)
    dk_ref[...] = jnp.zeros_like(dk_ref)
    dv_ref[...] = jnp.zeros_like(dv_ref)

    def turn_back(grad, here):
        return (grad * cos_ref[here, :] - swap_halves(grad) * sin_ref[here, :]).astype(bf16)

    for blk in range(blocks):
        low = max(0, blk - reach)
        span = (blk + 1 - low) * rows
        slot = pl.multiple_of((me ^ blk) * rows, rows)
        here = slice(blk * rows, (blk + 1) * rows)
        fill_bias(bias_ref, begin_ref, blk, low, rows)
        prodt_ref[...] = (
            do_ref[pl.ds(slot, rows), :].astype(f32) * o_ref[pl.ds(slot, rows), :].astype(f32)
        ).T
        for head in range(2 * pairs):
            pair = head // 2
            cols = slice(pair * LANES, (pair + 1) * LANES)
            mine = slice(head * HEAD_DIM, (head + 1) * HEAD_DIM)
            query = head_mask(q_ref[here, cols], head % 2) * jnp.asarray(scale, bf16)
            grad = head_mask(do_ref[pl.ds(slot, rows), cols], head % 2)
            delta = jnp.sum(prodt_ref[mine, :], axis=0, keepdims=True)
            lse = lse_ref[head : head + 1, here]
            for at in range(0, span, CHUNK):
                keys = slice(low * rows + at, low * rows + at + CHUNK)
                score = dot_nt(k_ref[keys, cols], query) + bias_ref[at : at + CHUNK, :]
                prob = jnp.exp(score - lse)
                dprob = dot_nt(v_ref[keys, cols], grad)
                prob_ref[at : at + CHUNK, :] = prob.astype(bf16)
                ds_ref[at : at + CHUNK, :] = (prob * (dprob - delta)).astype(bf16)
            reachable = slice(low * rows, low * rows + span)
            dv_ref[reachable, cols] += dot_nn(prob_ref[:span, :], grad)
            dk_ref[reachable, cols] += dot_nn(ds_ref[:span, :], query)
            dqt_ref[mine, :] = dot_nn(kt_ref[mine, reachable], ds_ref[:span, :]) * scale
        dquery = dqt_ref[...].T
        for pair in range(pairs):
            cols = slice(pair * LANES, (pair + 1) * LANES)
            dlin_ref[pl.ds(slot, rows), cols] = turn_back(dquery[:, cols], here)
    for blk in range(blocks):
        slot = pl.multiple_of((me ^ blk) * rows, rows)
        here = slice(blk * rows, (blk + 1) * rows)
        for pair in range(pairs):
            cols = slice(pair * LANES, (pair + 1) * LANES)
            keycols = slice(width + pair * LANES, width + (pair + 1) * LANES)
            dlin_ref[pl.ds(slot, rows), keycols] = turn_back(dk_ref[here, cols], here)
        dlin_ref[pl.ds(slot, rows), 2 * width :] = dv_ref[here, :].astype(bf16)


def attend_forward(lin, tables, me, rows, width, window):
    group = lin.shape[0]
    heads = width // HEAD_DIM
    whole = pl.BlockSpec(memory_space=pltpu.VMEM)
    span = min(group, window + rows)
    return pl.pallas_call(
        functools.partial(forward_kernel, rows, width, window),
        out_shape=(
            jax.ShapeDtypeStruct((group, width), bf16),
            jax.ShapeDtypeStruct((group, width), bf16),
            jax.ShapeDtypeStruct((group, width), bf16),
            jax.ShapeDtypeStruct((group, width), bf16),
            jax.ShapeDtypeStruct((heads, group), f32),
        ),
        in_specs=[pl.BlockSpec(memory_space=pltpu.SMEM)] + [whole] * 4,
        out_specs=(whole,) * 5,
        scratch_shapes=[
            pltpu.VMEM((width, group), bf16),
            pltpu.VMEM((span, rows), f32),
            pltpu.VMEM((span, rows), f32),
            pltpu.VMEM((span, rows), bf16),
            pltpu.VMEM((width, rows), f32),
        ],
        compiler_params=pltpu.CompilerParams(vmem_limit_bytes=48 * 1024 * 1024),
        name="attend_forward",
    )(me, lin, *tables)


def attend_backward(grad, mixed, saved, tables, me, rows, width, window):
    query, keys, values, lse = saved
    group = query.shape[0]
    whole = pl.BlockSpec(memory_space=pltpu.VMEM)
    span = min(group, window + rows)
    return pl.pallas_call(
        functools.partial(backward_kernel, rows, width, window),
        out_shape=jax.ShapeDtypeStruct((group, 3 * width), bf16),
        in_specs=[pl.BlockSpec(memory_space=pltpu.SMEM)] + [whole] * 9,
        out_specs=whole,
        scratch_shapes=[
            pltpu.VMEM((width, group), bf16),
            pltpu.VMEM((span, rows), f32),
            pltpu.VMEM((span, rows), bf16),
            pltpu.VMEM((span, rows), bf16),
            pltpu.VMEM((width, rows), f32),
            pltpu.VMEM((width, rows), f32),
            pltpu.VMEM((group, width), f32),
            pltpu.VMEM((group, width), f32),
        ],
        compiler_params=pltpu.CompilerParams(vmem_limit_bytes=48 * 1024 * 1024),
        name="attend_backward",
    )(me, grad, mixed, query, keys, values, lse, *tables)


def position_tables(seq_lengths, group):
    row_ids = jnp.arange(group, dtype=jnp.int32)
    ends = jnp.cumsum(seq_lengths)
    starts = ends - seq_lengths
    begins = jnp.max(jnp.where(starts[None, :] <= row_ids[:, None], starts[None, :], 0), axis=1)
    place = (row_ids - begins).astype(f32)
    half = ROT_DIM // 2
    lane = jnp.arange(LANES, dtype=jnp.int32) % HEAD_DIM
    frequency = jnp.exp((lane % half).astype(f32) * (-2.0 * math.log(10000.0) / ROT_DIM))
    lane_freq = jnp.where(lane < ROT_DIM, frequency, 0.0)
    sign = jnp.where(lane < half, -1.0, 1.0).astype(f32)
    angle = place[:, None] * lane_freq[None, :]
    return jnp.cos(angle), jnp.sin(angle) * sign[None, :], begins[None, :].astype(jnp.int32)


def swap_mp(array, offset):
    count = lax.axis_size("mp")
    return lax.ppermute(array, "mp", [(i, i ^ offset) for i in range(count)])


def swap_dp(array, offset):
    count = lax.axis_size("dp")
    return lax.ppermute(array, "dp", [(i, i ^ offset) for i in range(count)])


def tie(array, *after):
    return lax.optimization_barrier((array,) + after)[0]


def gather_pieces(piece):
    count = lax.axis_size("mp")
    pieces = [None] * count
    for chip in range(0, count, 2):
        pieces[chip] = piece if chip == 0 else swap_mp(piece, chip)
        pieces[chip + 1] = swap_mp(pieces[chip], 1)
    return pieces


def absolute_order(pieces, me):
    bit = 1
    while bit < len(pieces):
        flip = (me & bit) != 0
        pieces = [
            jnp.where(flip, pieces[i ^ bit], pieces[i]) for i in range(len(pieces))
        ]
        bit *= 2
    return pieces


def chip_sums(parts, chips):
    return {
        chip: parts[chip].astype(f32) + swap_mp(parts[chip + 1].astype(bf16), 1).astype(f32)
        for chip in chips
    }


class DpScatter:

    def __init__(self, grad, order=()):
        count = lax.axis_size("dp")
        self.left = list(range(count.bit_length() - 1))
        self.order = list(order) + [b for b in self.left if b not in order]
        self.came = None
        self.now = grad.reshape(count, grad.shape[0] // count, grad.shape[1])
        self.send()

    def send(self):
        bit = self.order.pop(0)
        low = 1 << self.left.index(bit)
        self.left.remove(bit)
        upper = ((lax.axis_index("dp") >> bit) & 1) != 0
        block = self.now.shape[1:]
        pairs = self.now.reshape((-1, 2, low) + block)
        first, second = pairs[:, 0].reshape((-1,) + block), pairs[:, 1].reshape((-1,) + block)
        self.keep = jnp.where(upper, second, first)
        going = jnp.where(upper, first, second)
        self.came = swap_dp(going, 1 << bit)

    def step(self, *after):
        if self.came is None:
            return
        came = tie(self.came, *after) if after else self.came
        self.now = self.keep.astype(f32) + came.astype(f32)
        self.came = None
        if self.order:
            self.now = self.now.astype(bf16)
            self.send()

    def total(self):
        while self.came is not None:
            self.step()
        return self.now[0]


def gelu_pair(pre):
    cdf = 0.5 * (1.0 + lax.erf(pre * (1.0 / math.sqrt(2.0))))
    density = jnp.exp(-0.5 * pre * pre) * (1.0 / math.sqrt(2.0 * math.pi))
    return (pre * cdf).astype(bf16), (cdf + pre * density).astype(bf16)


def shards(
    hidden_in, cotangent, lengths, ln_gain, ln_bias, qkv_weight, qkv_bias,
    out_weight, out_bias, fc_weight, fc_bias, proj_weight, proj_bias,
):
    count = lax.axis_size("mp")
    me = lax.axis_index("mp")
    rows, model = hidden_in.shape
    group = rows * count
    width = model // count
    window = group // 2
    me_vec = me.astype(jnp.int32).reshape(1)
    tables = position_tables(lengths[0], group)
    gain = ln_gain.astype(f32)
    shift = ln_bias.astype(f32)

    def layer_slice(array, layer, start, size):
        return lax.dynamic_slice(array, (layer,) + start, (1,) + size)[0]

    def own_cols(layer):
        return jnp.concatenate(
            [
                layer_slice(qkv_weight, layer, (0, part * model + me * width), (model, width))
                for part in range(3)
            ],
            axis=1,
        )

    def own_bias(layer):
        return jnp.concatenate(
            [
                layer_slice(qkv_bias, layer, (part * model + me * width,), (width,))
                for part in range(3)
            ]
        ).astype(f32)

    def out_rows(layer, k):
        return layer_slice(out_weight, layer, ((me ^ k) * width, 0), (width, model))

    wqkv, bqkv, wout_own, wout_rel = [], [], [], []
    for l in range(LAYERS):
        wqkv.append(own_cols(l))
        bqkv.append(own_bias(l))
        wout_own.append(out_rows(l, 0))
        wout_rel.append(jnp.concatenate([out_rows(l, k) for k in range(count)], axis=0))
    pair_rows = 2 * rows
    far_chips = range(2, count, 2)

    def split_rows(near, far):
        return [near[:rows], near[rows:]] + [
            far[i * rows : (i + 1) * rows] for i in range(count - 2)
        ]

    def fc_part(part, l):
        return gelu_pair(dot_nn(part, fc_weight[l]) + fc_bias[l].astype(f32))

    hidden = hidden_in
    saved = []
    stat_rows = []
    mixed_alls = [None] * LAYERS

    def finish_mixed(mixed, got, *after):
        mixed = tie(mixed, *after) if after else mixed
        full = []
        for k in range(0, count, 2):
            if k == 0:
                rest = mixed[pair_rows:]
            else:
                order = [mixed[(s ^ k) * rows : (s ^ k) * rows + 2 * rows] for s in far_chips]
                rest = swap_mp(jnp.concatenate(order, axis=0), k)
            tail = swap_mp(rest, 1)
            flipped = [got[k + 1][rows:], got[k + 1][:rows]]
            for s in range(0, count - 2, 2):
                flipped += [tail[(s + 1) * rows : (s + 2) * rows], tail[s * rows : (s + 1) * rows]]
            full += [jnp.concatenate([got[k], rest], axis=0), jnp.concatenate(flipped, axis=0)]
        return jnp.concatenate(full, axis=1)

    first_cots = []

    def send_branch(branch):
        away = {chip: swap_mp(branch, chip) for chip in far_chips}
        return branch, swap_mp(branch, 1), away

    def prepare_cots(l, pieces):
        near, far = jnp.concatenate(pieces[:2], axis=0), jnp.concatenate(pieces[2:], axis=0)
        dmix = dot_nt(jnp.concatenate([near, far], axis=0), wout_own[l]).astype(bf16)
        return near, far, dmix, column_slices(pieces)

    def column_slices(pieces):
        return [lax.dynamic_slice_in_dim(p, me * width, width, 1) for p in pieces]

    def forward(l, hidden):
        center, rstd = norm_stats(hidden)
        act = (center * rstd * gain[l] + shift[l]).astype(bf16)
        away = {chip: swap_mp(act, chip) for chip in far_chips}
        near = jnp.concatenate([act, swap_mp(act, 1)], axis=0)
        if l == 0:
            first_cots.extend(send_branch(cotangent.astype(bf16)))
            top_far = []
            for chip in far_chips:
                top_far += [first_cots[2][chip], swap_mp(first_cots[2][chip], 1)]
            first_cots.append(prepare_cots(LAYERS - 1, [first_cots[0], first_cots[1]] + top_far))
        gelu_near, slope_near = fc_part(near, l)
        pieces = []
        for chip in far_chips:
            arrived = tie(away[chip], gelu_near, wqkv[l], wout_rel[l], *tables[:2])
            pieces += [arrived, swap_mp(arrived, 1)]
        near_out = dot_nt(gelu_near, proj_weight[l]).astype(bf16)
        pieces[1] = tie(pieces[1], near_out)
        far = jnp.concatenate(pieces, axis=0)
        acts = jnp.concatenate([near, far], axis=0)
        gelu_far, slope_far = fc_part(far, l)
        far_out = dot_nt(gelu_far, proj_weight[l]).astype(bf16)
        outs = split_rows(near_out, far_out)
        sums = chip_sums(outs, far_chips)
        sending = {chip: sums[chip].astype(bf16) for chip in far_chips}
        returned = {chip: swap_mp(sending[chip], chip) for chip in far_chips}
        lin = dot_nn(tie(acts, *sending.values()), wqkv[l]) + bqkv[l]
        mixed, query, keys, values, lse = attend_forward(
            lin, tables, me_vec, rows, width, window
        )
        mix_near = mixed[:pair_rows]
        got = {}
        for chip in far_chips:
            got[chip] = swap_mp(mixed[chip * rows : (chip + 2) * rows], chip)
        got[0] = mix_near
        got[1] = swap_mp(mix_near, 1)
        ffn = chip_sums(outs, [0])[0] + proj_bias[l].astype(f32)
        for chip in far_chips:
            ffn = ffn + tie(returned[chip], mixed).astype(f32)
        base = hidden + ffn
        squares = [jnp.sum(hidden * hidden, axis=0), jnp.sum(ffn * ffn, axis=0)]
        for chip in far_chips:
            got[chip] = tie(got[chip], base)
            got[chip + 1] = swap_mp(got[chip], 1)
        own = [got[k][:rows] if k % 2 == 0 else got[k][rows:] for k in range(count)]
        attn = dot_nn(jnp.concatenate(own, axis=1), wout_rel[l]) + out_bias[l].astype(f32)
        stat_rows.append(jnp.stack([squares[0], jnp.sum(attn * attn, axis=0), squares[1]]))
        if l:
            mixed_alls[l - 1] = finish_mixed(*saved[l - 1][4], far_out)
        saved.append(
            (
                hidden, acts, mixed, (query, keys, values, lse), (mixed, got),
                (gelu_near, gelu_far), (slope_near, slope_far),
            )
        )
        return base + attn

    for l in range(LAYERS):
        hidden = forward(l, hidden)
    mixed_alls[-1] = finish_mixed(*saved[-1][4])

    grad_res = cotangent
    grads, late_fc = {}, []
    small_mp, small_dp = [None] * LAYERS, [None] * LAYERS

    def advance(layer, names, *after):
        if layer < LAYERS:
            for name in names:
                grads[name, layer].step(*after)

    def backward(l, grad_res):
        hidden_l, acts, mixed, heads, _, gelu, slope = saved[l]
        mixed_all = mixed_alls[l]
        if l == LAYERS - 1:
            branch, _, _, (near, far, dmix, own_cots) = first_cots
            dpre_near = (dot_nn(near, proj_weight[l]) * slope[0].astype(f32)).astype(bf16)
        else:
            branch, beside, away = send_branch(grad_res.astype(bf16))
            near = jnp.concatenate([branch, beside], axis=0)
            dpre_near = (dot_nn(near, proj_weight[l]) * slope[0].astype(f32)).astype(bf16)
            late_acts, late_near, late_far = late_fc.pop()
            late_acts = tie(late_acts, branch)
            fc_grad = (
                dot_tn(late_acts[:pair_rows], late_near)
                + dot_tn(late_acts[pair_rows:], late_far)
            ).astype(bf16)
            grads[FC, l + 1] = DpScatter(fc_grad)
            advance(l + 1, [OUT], fc_grad)
            dpre_near = tie(dpre_near, fc_grad)
            far_pieces = []
            for chip in far_chips:
                arrived = tie(away[chip], dpre_near)
                far_pieces += [arrived, swap_mp(arrived, 1)]
            far = jnp.concatenate(far_pieces, axis=0)
            dmix = dot_nt(jnp.concatenate([near, far], axis=0), wout_own[l]).astype(bf16)
            own_cots = None
        dpre_far = (dot_nn(far, proj_weight[l]) * slope[1].astype(f32)).astype(bf16)
        advance(l + 1, [PROJ, QKV, OUT], dpre_far)
        proj_grad = (dot_tn(near, gelu[0]) + dot_tn(far, gelu[1])).astype(bf16)
        if l:
            grads[PROJ, l] = DpScatter(proj_grad)
            late_fc.append((acts, dpre_near, dpre_far))
        else:
            fc_grad = (
                dot_tn(acts[:pair_rows], dpre_near) + dot_tn(acts[pair_rows:], dpre_far)
            ).astype(bf16)
            grads[FC, l] = DpScatter(fc_grad)
            grads[PROJ, l] = DpScatter(proj_grad)
            advance(l + 1, [FC], proj_grad)
        dlin = attend_backward(dmix, mixed, heads, tables, me_vec, rows, width, window)
        far_da = (dot_nt(dpre_far, fc_weight[l]) + dot_nt(dlin[pair_rows:], wqkv[l])).astype(bf16)
        sums = chip_sums([None, None] + split_rows(far_da, far_da)[2:], far_chips)
        sending = {chip: sums[chip].astype(bf16) for chip in far_chips}
        returned = {chip: swap_mp(sending[chip], chip) for chip in far_chips}
        advance(l + 1, [FC], *sending.values())
        advance(l, [FC] if l == 0 else [PROJ], *sending.values())
        dlin_late = tie(dlin, *sending.values())
        qkv_grad = dot_tn(acts, dlin_late).astype(bf16)
        grads[QKV, l] = DpScatter(qkv_grad)
        near_da = (
            dot_nt(dpre_near, fc_weight[l]) + dot_nt(tie(dlin, qkv_grad)[:pair_rows], wqkv[l])
        ).astype(bf16)
        advance(l + 1, [QKV, OUT], near_da)
        if l == 0:
            advance(l, [PROJ], near_da)
        if l == 0:
            advance(l, [FC], qkv_grad)
        if own_cots is None:
            late = lax.optimization_barrier(([branch, beside] + far_pieces, qkv_grad))[0]
            own_cots = column_slices(late)
        else:
            own_cots = lax.optimization_barrier((own_cots, qkv_grad))[0]
        own_cots = jnp.concatenate(own_cots, axis=0)
        out_rel = dot_tn(mixed_all, own_cots).astype(bf16)
        out_abs = jnp.concatenate(
            absolute_order([out_rel[k * width : (k + 1) * width] for k in range(count)], me), axis=0
        )
        grads[OUT, l] = DpScatter(out_abs)
        advance(l + 1, [FC], out_abs)
        if l:
            advance(l, [PROJ], out_abs)
        dact = chip_sums([near_da[:rows], near_da[rows:]], [0])[0]
        for chip in far_chips:
            dact = dact + tie(returned[chip], out_abs).astype(f32)
        advance(l, [QKV] if l else [QKV, OUT, PROJ], dact)
        center, rstd = norm_stats(hidden_l)
        normed = center * rstd
        dnormed = dact * gain[l]
        dhidden = rstd * (
            dnormed
            - jnp.mean(dnormed, axis=-1, keepdims=True)
            - normed * jnp.mean(dnormed * normed, axis=-1, keepdims=True)
        )
        gain_sum = jnp.sum(dact * normed, axis=0)
        grad_below = grad_res + dhidden
        qkvb = jnp.sum(dlin.astype(f32), axis=0).reshape(3, width)
        qkvb_rows = lax.dynamic_update_slice_in_dim(
            jnp.zeros((3, model), f32), qkvb, me * width, 1
        )
        fcb = jnp.sum(dpre_near.astype(f32), axis=0) + jnp.sum(dpre_far.astype(f32), axis=0)
        small_mp[l] = jnp.concatenate(
            [
                gain_sum[None],
                jnp.sum(dact, axis=0)[None],
                jnp.sum(branch.astype(f32), axis=0)[None],
                qkvb_rows,
                stat_rows[l],
            ],
            axis=0,
        )
        small_dp[l] = jnp.pad(fcb, (0, -fcb.shape[0] % model)).reshape(-1, model)
        return grad_below

    for l in reversed(range(LAYERS)):
        grad_res = backward(l, grad_res)
    lines = small_mp[0].shape[0]
    sums = jnp.concatenate(small_mp, axis=0)
    step = 1
    while step < count:
        sums = sums + swap_mp(sums, step)
        step *= 2
    sums = jnp.concatenate([sums] + small_dp, axis=0)
    step = 1
    while step < lax.axis_size("dp"):
        sums = sums + swap_dp(sums, step)
        step *= 2
    advance(0, [QKV, OUT], sums)
    small = [sums[l * lines : (l + 1) * lines] for l in range(LAYERS)]
    fcb_rows = sums[LAYERS * lines :].reshape(LAYERS, -1)
    qkv_total, outw_total = [], []
    for l in range(LAYERS):
        both = jnp.concatenate(
            [grads[QKV, l].total().astype(bf16), grads[OUT, l].total().astype(bf16)], axis=1
        )
        pieces = absolute_order(gather_pieces(both), me)
        qkv_total.append(
            jnp.concatenate(
                [p[:, part * width : (part + 1) * width] for part in range(3) for p in pieces],
                axis=1,
            ).astype(f32)
        )
        outw_total.append(jnp.concatenate([p[:, 3 * width :] for p in pieces], axis=1).astype(f32))
    entries = float(rows * lax.axis_size("dp") * count * model)
    outb = jnp.stack([s[2] for s in small])
    return (
        hidden,
        grad_res,
        jnp.sqrt(jnp.stack([jnp.sum(s[6:9], axis=1) for s in small]) / entries),
        jnp.stack([s[0] for s in small]),
        jnp.stack([s[1] for s in small]),
        jnp.stack(qkv_total),
        jnp.stack([s[3:6].reshape(-1) for s in small]),
        jnp.stack(outw_total),
        outb,
        jnp.stack([grads[FC, l].total() for l in range(LAYERS)]),
        fcb_rows[:, : fc_bias.shape[1]],
        jnp.stack([grads[PROJ, l].total() for l in range(LAYERS)]),
        outb,
    )


def solution(mesh):
    tokens = P(("dp", "mp"), None)
    hidden_units = P(None, None, "mp")
    return jax.shard_map(
        shards,
        mesh=mesh,
        in_specs=(
            tokens, tokens, P("dp", None), P(), P(), P(), P(), P(), P(),
            hidden_units, P(None, "mp"), hidden_units, P(),
        ),
        out_specs=(
            tokens, tokens, P(), P(), P(), P(None, "dp", None), P(), P(None, "dp", None), P(),
            P(None, "dp", "mp"), P(None, "mp"), P(None, "dp", "mp"), P(),
        ),
        check_vma=False,
    )
```
